128 devices in a mesh: req: 4 (over z), seq: 32 (over x, y, core).
Axes of the slice: x: 4, y: 4, z: 4, core: 2. Of those that a mesh axis runs over, the one named last changes fastest.
Arguments:
- tokens: bfloat16 [4, 2048, 3584], P('req', 'seq'), may hold values from -6 to 6
- w_z: bfloat16 [3584, 7168], P('req', 'seq')
- w_x: bfloat16 [3584, 7168], P('req', 'seq'), may hold values from -0.09375 to 0.09375
- w_bc: bfloat16 [3584, 256], replicated, may hold values from -0.09375 to 0.09375
- w_dt: bfloat16 [3584, 112], replicated, may hold values from -0.09375 to 0.09375
- dt_bias: float32 [112], replicated, may hold values from -2 to 0
- a_rate: float32 [112], replicated, may hold values from 0.00024414062 to 0.2
- conv_weight: float32 [4, 7424], replicated, may hold values from -3 to 3
- conv_bias: float32 [7424], replicated, may hold values from -3 to 3
- d_skip: float32 [112], replicated, may hold values from 0.5 to 1.5
- norm_gain: float32 [7168], replicated, may hold values from 0.5 to 1.5
- lengths: int32 [4], P('req'), may hold values from 512 to 2048, as said below
Outputs:
- mixed: bfloat16 [4, 2048, 7168], P('req', 'seq')
The draws below stay inside these ranges and needn't reach their ends.
Inputs may be any that keep to these rules, and one draw needn't show every extreme that they name: `lengths`: each prompt has at least 512 valid positions, and the longest fills all 2048.
All inputs are finite; a program needn't handle non-finite values.
Results may differ from the reference program's by a relative error of at most 0.0055.
Values may be sent and summed in bfloat16 or wider, within the bound.
No kernel may reach another device: no remote copies, remote signals or barrier semaphores. Data moves between devices by JAX's collectives and lax.ppermute only.
A program may use at most 320 MiB of HBM per device.

```python
import math
import jax
import jax.numpy as jnp
from jax import lax

D = 3584
INNER = 7168
HEADS = 112
HEAD = 64
STATE = 64
GROUPS = 2
CONV = 4
TOK_DEV = 64
REQS = 4
LEN = 2048
XBC = 7424


def draw_lengths(key, part):
    first_key, second_key = jax.random.split(jax.random.fold_in(key, 11))
    drawn = jax.random.randint(first_key, (REQS,), LEN // 4, LEN + 1)
    longest = jax.random.randint(second_key, (), 0, REQS)
    return jnp.where(jnp.arange(REQS) == longest, LEN, drawn).astype(jnp.int32)


def draw_w_z(key, part):
    own_key = jax.random.fold_in(key, 5)
    group_width = INNER // GROUPS
    position = (jnp.arange(INNER) % group_width).astype(jnp.float32) / group_width
    base = jnp.clip(jax.random.normal(own_key, (D, INNER), jnp.float32), -6.0, 6.0)
    scale = 3.0 ** position
    return (base * scale[None, :] * D ** (-0.5)).astype(jnp.bfloat16)


def steps_of(rng, shape, cuts, low, largest):
    loudness, own = 1.0, jax.random.fold_in(rng, 6)
    for dim, parts in cuts:
        heights = jnp.exp(jax.random.uniform(jax.random.fold_in(own, dim), (parts,), jnp.float32, low / len(cuts), largest / len(cuts)))
        loudness = loudness * jnp.repeat(heights, shape[dim] // parts).reshape([-1 if axis == dim else 1 for axis in range(len(shape))])
    return loudness


def scatter_about(rng, extent, width, most, cuts=(), kind=jnp.bfloat16):
    array = width * jax.random.normal(rng, extent, jnp.float32)
    if cuts:
        array = array * steps_of(rng, extent, cuts, -0.22, 0.18)
    return jnp.clip(array, -most, most).astype(kind)


def setup_inputs(seed: int = 0) -> dict:
    arg_keys = jax.random.split(jax.random.key(seed), 13)
    return {
        "tokens": scatter_about(arg_keys[0], (REQS, LEN, D), 1.0, 6.0, ((0, 4), (1, 32))),
        "w_z": draw_w_z(jax.random.fold_in(arg_keys[12], 71), 0),
        "w_x": scatter_about(arg_keys[2], (D, INNER), D ** -0.5, 0.09375, ((0, 4), (1, 32))),
        "w_bc": scatter_about(arg_keys[3], (D, 2 * GROUPS * STATE), D ** -0.5, 0.09375),
        "w_dt": scatter_about(arg_keys[4], (D, HEADS), D ** -0.5, 0.09375),
        "dt_bias": jnp.clip(jax.random.uniform(arg_keys[5], (HEADS,), jnp.float32, -2.0, 0.0), -2.0, 0.0),
        "a_rate": jnp.clip(jnp.exp(jax.random.uniform(arg_keys[6], (HEADS,), jnp.float32, math.log(0.00024414062), math.log(0.2))), 0.00024414062, 0.2),
        "conv_weight": scatter_about(arg_keys[7], (CONV, XBC), CONV ** -0.5, 3.0, (), jnp.float32),
        "conv_bias": scatter_about(arg_keys[8], (XBC,), 0.5, 3.0, (), jnp.float32),
        "d_skip": jnp.clip(jax.random.uniform(arg_keys[9], (HEADS,), jnp.float32, 0.5, 1.5), 0.5, 1.5),
        "norm_gain": jnp.clip(1.0 + 0.1 * jax.random.normal(arg_keys[10], (INNER,), jnp.float32), 0.5, 1.5),
        "lengths": draw_lengths(jax.random.fold_in(arg_keys[12], 71), 0),
    }


PRECISE = lax.Precision.HIGHEST

def block_scan(x_heads, b_proj, c_proj, step_size, log_decay, state_in):
    per_group = x_heads.shape[1] // b_proj.shape[1]
    block_len = x_heads.shape[0]
    running = jnp.cumsum(log_decay, axis=0)
    causal_mask = jnp.arange(block_len)[:, None] >= jnp.arange(block_len)[None, :]
    gaps = running.T[:, :, None] - running.T[:, None, :]
    decay_mask = jnp.where(causal_mask[None], jnp.exp(jnp.minimum(gaps, 0.0)), 0.0)
    affinity = jnp.einsum('ign,jgn->gij', c_proj, b_proj, precision=PRECISE)
    mixing = decay_mask * jnp.repeat(affinity, per_group, axis=0) * step_size.T[:, None, :]
    intra_out = jnp.einsum('hij,jhp->ihp', mixing, x_heads, precision=PRECISE)
    c_heads = jnp.repeat(c_proj, per_group, axis=1)
    b_heads = jnp.repeat(b_proj, per_group, axis=1)
    carried = jnp.exp(running)[:, :, None] * jnp.einsum('ihn,hpn->ihp', c_heads, state_in, precision=PRECISE)
    tail_weight = jnp.exp(running[-1][None, :] - running) * step_size
    block_state = jnp.einsum('jhp,jhn->hpn', x_heads * tail_weight[:, :, None], b_heads, precision=PRECISE)
    return (intra_out + carried, block_state, running[-1])

def reference(tokens, w_z, w_x, w_bc, w_dt, dt_bias, a_rate, conv_weight, conv_bias, d_skip, norm_gain, lengths):

    def one_prompt(operands):
        prompt_tokens, length = operands
        gate_in = jnp.dot(prompt_tokens, w_z, preferred_element_type=jnp.float32).astype(jnp.bfloat16)
        x_in = jnp.dot(prompt_tokens, w_x, preferred_element_type=jnp.float32).astype(jnp.bfloat16)
        bc_proj = jnp.dot(prompt_tokens, w_bc, preferred_element_type=jnp.float32).astype(jnp.bfloat16)
        dt_raw = jnp.dot(prompt_tokens, w_dt, preferred_element_type=jnp.float32).astype(jnp.bfloat16)
        xbc = jnp.concatenate([x_in, bc_proj], axis=1)
        padded = jnp.pad(xbc.astype(jnp.float32), ((CONV - 1, 0), (0, 0)))
        conv_sum = conv_bias[None, :] + jnp.zeros((LEN, XBC), jnp.float32)
        for offset in range(CONV):
            conv_sum = conv_sum + conv_weight[offset][None, :] * padded[offset:offset + LEN]
        conved = lax.optimization_barrier(jax.nn.silu(conv_sum).astype(jnp.bfloat16)).astype(jnp.float32)
        x_heads = conved[:, :INNER].reshape(LEN, HEADS, HEAD)
        b_proj = conved[:, INNER:INNER + GROUPS * STATE].reshape(LEN, GROUPS, STATE)
        c_proj = conved[:, INNER + GROUPS * STATE:].reshape(LEN, GROUPS, STATE)
        step_size = jax.nn.softplus(dt_raw.astype(jnp.float32) + dt_bias[None, :])
        log_decay = -step_size * a_rate[None, :]
        blocks = LEN // TOK_DEV

        def advance(state_in, pieces):
            x_block, b_block, c_block, size_block, decay_block = pieces
            result, block_state, total_log = block_scan(x_block, b_block, c_block, size_block, decay_block, state_in)
            return (jnp.exp(total_log)[:, None, None] * state_in + block_state, result)
        final_state, results = lax.scan(advance, jnp.zeros((HEADS, HEAD, STATE), jnp.float32), (x_heads.reshape(blocks, TOK_DEV, HEADS, HEAD), b_proj.reshape(blocks, TOK_DEV, GROUPS, STATE), c_proj.reshape(blocks, TOK_DEV, GROUPS, STATE), step_size.reshape(blocks, TOK_DEV, HEADS), log_decay.reshape(blocks, TOK_DEV, HEADS)))
        result = results.reshape(LEN, HEADS, HEAD) + d_skip[None, :, None] * x_heads
        gated = result.reshape(LEN, INNER) * jax.nn.silu(gate_in.astype(jnp.float32))
        grouped = gated.reshape(LEN, GROUPS, INNER // GROUPS)
        inv_scale = lax.rsqrt(lax.optimization_barrier(jnp.mean(grouped * grouped, axis=2, keepdims=True)) + 1e-05)
        normed = (grouped * inv_scale).reshape(LEN, INNER) * norm_gain[None, :]
        valid_rows = jnp.arange(LEN, dtype=jnp.int32) < length
        return jnp.where(valid_rows[:, None], normed, 0.0).astype(jnp.bfloat16)
    return lax.map(one_prompt, (tokens, lengths))
```

```python
import functools

import jax
import jax.numpy as jnp
from jax import lax
from jax.experimental import pallas as pl
from jax.experimental.pallas import tpu as pltpu
from jax.sharding import PartitionSpec as P

GROUPS = 2
STATE = 64
HEAD = 64
TILE = 128
SLOT = 256
PIECES = 4


def split(value):
    high = value.astype(jnp.bfloat16)
    return high, (value - high.astype(jnp.float32)).astype(jnp.bfloat16)


def matmul(a, b, dims=((1,), (0,))):
    return lax.dot_general(a, b, (dims, ((), ())), preferred_element_type=jnp.float32)


def scan_kernel(*refs):
    projected = refs[:PIECES]
    taps, conv_bias, head_rows, skip, out, xbc, state = refs[PIECES:]
    step = pl.program_id(0)
    rows = projected[0].shape[1]
    own = rows * PIECES
    past = xbc.shape[0] - TILE

    @pl.when(step == 0)
    def _():
        xbc[...] = jnp.zeros_like(xbc)
        state[...] = jnp.zeros_like(state)

    @pl.when(step > 0)
    def _():
        xbc[0:past] = xbc[TILE : TILE + past]

    gates = []
    for owner in range(TILE // own):
        for piece in range(PIECES):
            block = projected[piece][owner]
            start = past + owner * own + piece * rows
            xbc[start : start + rows, :SLOT] = block[:, :SLOT].astype(jnp.float32)
            xbc[start : start + rows, SLOT:] = block[:, 2 * SLOT :].astype(jnp.float32)
            gates.append(block[:, SLOT : 2 * SLOT])
    gate = jnp.concatenate(gates, axis=0).astype(jnp.float32)

    total = conv_bias[...]
    count = taps.shape[0]
    for k in range(count):
        first = past - (count - 1) + k
        total = total + taps[k : k + 1] * xbc[first : first + TILE]
    conved = (total * jax.nn.sigmoid(total)).astype(jnp.bfloat16)
    b_proj = conved[:, SLOT : SLOT + TILE]
    c_proj = conved[:, SLOT + TILE :]

    raw = xbc[past : past + TILE, SLOT + TILE :]
    step_size = jax.nn.softplus(raw + head_rows[0:1])
    log_decay = -step_size * head_rows[1:2]
    row = lax.broadcasted_iota(jnp.int32, (TILE, TILE), 0)
    lane = lax.broadcasted_iota(jnp.int32, (TILE, TILE), 1)
    causal = row >= lane
    running = jnp.dot(
        causal.astype(jnp.float32),
        log_decay,
        precision=lax.Precision.HIGHEST,
        preferred_element_type=jnp.float32,
    )
    running_rows = running.T
    step_rows = step_size.T
    affinity = jnp.where(causal, matmul(c_proj, b_proj, ((1,), (1,))), 0.0)
    before = state[...]
    before_high, before_low = split(before)
    carried = matmul(c_proj, before_high) + matmul(c_proj, before_low)

    left = lane < HEAD
    for tile in range(SLOT // TILE):
        span = slice(tile * TILE, (tile + 1) * TILE)
        x = conved[:, span]
        mixing, columns, steps = [], [], []
        for half in range(2):
            at = STATE + 2 * tile + half
            column = jnp.broadcast_to(running[:, at : at + 1], (TILE, TILE))
            decay = jnp.exp(jnp.minimum(column - running_rows[at : at + 1], 0.0))
            mixing.append(decay * affinity * step_rows[at : at + 1])
            columns.append(column)
            steps.append(jnp.broadcast_to(step_size[:, at : at + 1], (TILE, TILE)))
        weights, rest = split(jnp.concatenate(mixing, axis=1))
        zero = jnp.zeros_like(x)
        values = jnp.concatenate([jnp.where(left, x, zero), jnp.where(left, zero, x)], axis=0)
        intra = matmul(weights, values) + matmul(rest, values)
        run = jnp.where(left, columns[0], columns[1])
        last = run[TILE - 1 :]
        x32 = x.astype(jnp.float32)
        result = intra + jnp.exp(run) * carried[:, span] + skip[:, span] * x32
        z = gate[:, span]
        gated = (result * (z * jax.nn.sigmoid(z))).astype(jnp.bfloat16)
        width = min(out.shape[2] - tile * TILE, TILE)
        for owner in range(TILE // own):
            out[owner, :, tile * TILE : tile * TILE + width] = gated[
                owner * own : (owner + 1) * own, :width
            ]
        added = x32 * (jnp.exp(last - run) * jnp.where(left, steps[0], steps[1]))
        added_high, added_low = split(added)
        block = matmul(b_proj, added_high, ((0,), (0,))) + matmul(b_proj, added_low, ((0,), (0,)))
        state[:, span] = jnp.exp(last) * before[:, span] + block


def scan(projected, taps, conv_bias, head_rows, skip, width):
    owners, rows, columns = projected[0].shape
    own = rows * PIECES
    per_step = TILE // own
    whole = lambda array: pl.BlockSpec(array.shape, lambda i: (0,) * array.ndim)
    constants = (taps, conv_bias, head_rows, skip)
    return pl.pallas_call(
        scan_kernel,
        grid=(owners // per_step,),
        in_specs=[pl.BlockSpec((per_step, rows, columns), lambda i: (i, 0, 0))] * PIECES
        + [whole(array) for array in constants],
        out_specs=pl.BlockSpec((per_step, own, width), lambda i: (i, 0, 0)),
        out_shape=jax.ShapeDtypeStruct((owners, own, width), jnp.bfloat16),
        scratch_shapes=[
            pltpu.VMEM((TILE + 8, 2 * SLOT), jnp.float32),
            pltpu.VMEM((TILE, SLOT), jnp.float32),
        ],
        name="mixer_scan",
    )(*projected, *constants)


def norm_kernel(turned, limit, gated, gain, out):
    owners, rows, width = gated.shape
    per_group = owners // GROUPS
    position = lax.broadcasted_iota(jnp.int32, (rows, 1), 0)
    valid = position < limit[0]
    for group in range(GROUPS):
        members = range(group * per_group, (group + 1) * per_group)
        squares = jnp.zeros((rows, width), jnp.float32)
        for owner in members:
            block = gated[owner].astype(jnp.float32)
            squares = squares + block * block
        mean = jnp.sum(squares, axis=1, keepdims=True) * (1.0 / (per_group * width))
        scale = jnp.where(valid, lax.rsqrt(mean + 1e-05), 0.0)
        for owner in members:
            block = gated[owner].astype(jnp.float32) * scale * gain[owner : owner + 1]
            block = jnp.where(valid, block, 0.0).astype(jnp.bfloat16)
            start = owner * width
            if owner % 2 == 0:
                out[:, start : start + width] = block
            else:
                out[:, start + turned : start + width] = block[:, : width - turned]
                out[:, start : start + turned] = block[:, width - turned :]


def norm(limit, gated, gain, turned):
    owners, rows, width = gated.shape
    return pl.pallas_call(
        functools.partial(norm_kernel, turned),
        in_specs=[
            pl.BlockSpec(memory_space=pltpu.SMEM),
            pl.BlockSpec(memory_space=pltpu.VMEM),
            pl.BlockSpec(memory_space=pltpu.VMEM),
        ],
        out_specs=pl.BlockSpec(memory_space=pltpu.VMEM),
        out_shape=jax.ShapeDtypeStruct((rows, owners * width), jnp.bfloat16),
        name="gated_norm",
    )(limit, gated, gain)


def around(block, axis, distance):
    size = lax.axis_size(axis)
    return lax.ppermute(block, axis, [(i, (i + distance) % size) for i in range(size)])


def gather_rows(block, axis):
    depth = block.shape[0]
    half = depth // 2
    behind, ahead = around(block, axis, 1), around(block, axis, -1)
    far = jnp.concatenate(
        [around(behind[:half], axis, 1), around(ahead[half:], axis, -1)], axis=0
    )
    me = lax.axis_index(axis)
    whole = jnp.zeros((4 * depth,) + block.shape[1:], block.dtype)
    for distance, part in ((0, block), (3, behind), (1, ahead), (2, far)):
        whole = lax.dynamic_update_slice(whole, part, ((me + distance) % 4 * depth, 0))
    return whole


def local(
    tokens,
    w_z,
    w_x,
    w_bc,
    w_dt,
    dt_bias,
    a_rate,
    conv_weight,
    conv_bias,
    d_skip,
    norm_gain,
    lengths,
):
    own_rows = tokens[0]
    num_rows, depth = own_rows.shape
    width = w_x.shape[1]
    me = lax.axis_index("seq")
    owners = lax.axis_size("seq")
    odd = me % 2 == 1
    chip_heads = 2 * width // HEAD
    turned = width - 3 * HEAD
    inner = norm_gain.shape[0]
    group = me // (owners // GROUPS)

    rows = num_rows // PIECES
    token_pieces = [
        lax.all_gather(own_rows[j * rows : (j + 1) * rows], "seq") for j in range(PIECES)
    ]

    def turn(columns):
        return jnp.where(odd, jnp.roll(columns, -turned, axis=-1), columns)

    def pad(array, size):
        return jnp.pad(array, ((0, 0), (0, size - array.shape[-1])))

    def heads_of(array):
        chip = lax.dynamic_slice_in_dim(array, me // 2 * chip_heads, chip_heads, -1)
        return jnp.where(
            odd, jnp.concatenate([chip[..., 4:7], chip[..., 3:4]], axis=-1), chip[..., :4]
        )

    def states_of(array, start):
        first = lax.dynamic_slice_in_dim(array, start + group * STATE, STATE, -1)
        second = lax.dynamic_slice_in_dim(
            array, start + (GROUPS + group) * STATE, STATE, -1
        )
        return first, second

    both = gather_rows(jnp.concatenate([turn(w_x), turn(w_z)], axis=1), "req")
    w_b, w_c = states_of(w_bc, 0)
    weights = jnp.concatenate(
        [
            pad(both[:, :width], SLOT),
            pad(both[:, width:], SLOT),
            pad(w_b, TILE),
            pad(jnp.concatenate([w_c, heads_of(w_dt)], axis=1), TILE),
        ],
        axis=1,
    )

    def channels_of(array):
        x_part = turn(lax.dynamic_slice_in_dim(array, me * width, width, -1))
        b_part, c_part = states_of(array, inner)
        return jnp.concatenate([pad(x_part, SLOT), pad(b_part, TILE), pad(c_part, TILE)], axis=1)

    taps = channels_of(conv_weight)
    bias = channels_of(conv_bias[None])
    head_rows = jnp.pad(
        jnp.stack([heads_of(dt_bias), heads_of(a_rate)]), ((0, 0), (STATE, TILE - STATE - 4))
    )
    skip = jnp.repeat(heads_of(d_skip), HEAD)[None]
    gains = norm_gain.reshape(owners, width)
    gains = jnp.where(
        (jnp.arange(owners) % 2 == 1)[:, None], jnp.roll(gains, -turned, axis=1), gains
    )

    projected = []
    for piece in token_pieces:
        block = jnp.dot(
            piece.reshape(owners * rows, depth), weights, preferred_element_type=jnp.float32
        ).astype(jnp.bfloat16)
        projected.append(block.reshape(owners, rows, -1))
    gated = scan(projected, taps, bias, head_rows, skip, width)
    mine = lax.all_to_all(gated, "seq", split_axis=0, concat_axis=0, tiled=True)
    limit = lengths - me * num_rows
    return norm(limit, mine, gains, turned)[None]


def solution(mesh):
    placed = (
        P("req", "seq", None),
        P("req", "seq"),
        P("req", "seq"),
        P(),
        P(),
        P(),
        P(),
        P(),
        P(),
        P(),
        P(),
        P("req"),
    )
    return jax.shard_map(
        local, mesh=mesh, in_specs=placed, out_specs=P("req", "seq", None), check_vma=False
    )
```

```python
import functools

import jax
import jax.numpy as jnp
from jax import lax
from jax.experimental import pallas as pl
from jax.experimental.pallas import tpu as pltpu
from jax.sharding import PartitionSpec as P

GROUPS = 2
STATE = 64
HEAD = 64
TILE = 128
SLOT = 256
PIECES = 1


def split(value):
    high = value.astype(jnp.bfloat16)
    return high, (value - high.astype(jnp.float32)).astype(jnp.bfloat16)


def matmul(a, b, dims=((1,), (0,))):
    return lax.dot_general(a, b, (dims, ((), ())), preferred_element_type=jnp.float32)


def scan_kernel(*refs):
    projected = refs[:PIECES]
    taps, conv_bias, head_rows, skip, out, xbc, state = refs[PIECES:]
    step = pl.program_id(0)
    rows = projected[0].shape[1]
    own = rows * PIECES
    past = xbc.shape[0] - TILE

    @pl.when(step == 0)
    def _():
        xbc[...] = jnp.zeros_like(xbc)
        state[...] = jnp.zeros_like(state)

    @pl.when(step > 0)
    def _():
        xbc[0:past] = xbc[TILE : TILE + past]

    gates = []
    for owner in range(TILE // own):
        for piece in range(PIECES):
            block = projected[piece][owner]
            start = past + owner * own + piece * rows
            xbc[start : start + rows, :SLOT] = block[:, :SLOT].astype(jnp.float32)
            xbc[start : start + rows, SLOT:] = block[:, 2 * SLOT :].astype(jnp.float32)
            gates.append(block[:, SLOT : 2 * SLOT])
    gate = jnp.concatenate(gates, axis=0).astype(jnp.float32)

    total = conv_bias[...]
    count = taps.shape[0]
    for k in range(count):
        first = past - (count - 1) + k
        total = total + taps[k : k + 1] * xbc[first : first + TILE]
    conved = (total * jax.nn.sigmoid(total)).astype(jnp.bfloat16)
    b_proj = conved[:, SLOT : SLOT + TILE]
    c_proj = conved[:, SLOT + TILE :]

    raw = xbc[past : past + TILE, SLOT + TILE :]
    step_size = jax.nn.softplus(raw + head_rows[0:1])
    log_decay = -step_size * head_rows[1:2]
    row = lax.broadcasted_iota(jnp.int32, (TILE, TILE), 0)
    lane = lax.broadcasted_iota(jnp.int32, (TILE, TILE), 1)
    causal = row >= lane
    running = jnp.dot(
        causal.astype(jnp.float32),
        log_decay,
        precision=lax.Precision.HIGHEST,
        preferred_element_type=jnp.float32,
    )
    running_rows = running.T
    step_rows = step_size.T
    affinity = jnp.where(causal, matmul(c_proj, b_proj, ((1,), (1,))), 0.0)
    before = state[...]
    before_high, before_low = split(before)
    carried = matmul(c_proj, before_high) + matmul(c_proj, before_low)

    left = lane < HEAD
    for tile in range(SLOT // TILE):
        span = slice(tile * TILE, (tile + 1) * TILE)
        x = conved[:, span]
        mixing, columns, steps = [], [], []
        for half in range(2):
            at = STATE + 2 * tile + half
            column = jnp.broadcast_to(running[:, at : at + 1], (TILE, TILE))
            decay = jnp.exp(jnp.minimum(column - running_rows[at : at + 1], 0.0))
            mixing.append(decay * affinity * step_rows[at : at + 1])
            columns.append(column)
            steps.append(jnp.broadcast_to(step_size[:, at : at + 1], (TILE, TILE)))
        weights, rest = split(jnp.concatenate(mixing, axis=1))
        zero = jnp.zeros_like(x)
        values = jnp.concatenate([jnp.where(left, x, zero), jnp.where(left, zero, x)], axis=0)
        intra = matmul(weights, values) + matmul(rest, values)
        run = jnp.where(left, columns[0], columns[1])
        last = run[TILE - 1 :]
        x32 = x.astype(jnp.float32)
        result = intra + jnp.exp(run) * carried[:, span] + skip[:, span] * x32
        z = gate[:, span]
        gated = (result * (z * jax.nn.sigmoid(z))).astype(jnp.bfloat16)
        width = min(out.shape[2] - tile * TILE, TILE)
        for owner in range(TILE // own):
            out[owner, :, tile * TILE : tile * TILE + width] = gated[
                owner * own : (owner + 1) * own, :width
            ]
        added = x32 * (jnp.exp(last - run) * jnp.where(left, steps[0], steps[1]))
        added_high, added_low = split(added)
        block = matmul(b_proj, added_high, ((0,), (0,))) + matmul(b_proj, added_low, ((0,), (0,)))
        state[:, span] = jnp.exp(last) * before[:, span] + block


def scan(projected, taps, conv_bias, head_rows, skip, width):
    owners, rows, columns = projected[0].shape
    own = rows * PIECES
    per_step = TILE // own
    whole = lambda array: pl.BlockSpec(array.shape, lambda i: (0,) * array.ndim)
    constants = (taps, conv_bias, head_rows, skip)
    return pl.pallas_call(
        scan_kernel,
        grid=(owners // per_step,),
        in_specs=[pl.BlockSpec((per_step, rows, columns), lambda i: (i, 0, 0))] * PIECES
        + [whole(array) for array in constants],
        out_specs=pl.BlockSpec((per_step, own, width), lambda i: (i, 0, 0)),
        out_shape=jax.ShapeDtypeStruct((owners, own, width), jnp.bfloat16),
        scratch_shapes=[
            pltpu.VMEM((TILE + 8, 2 * SLOT), jnp.float32),
            pltpu.VMEM((TILE, SLOT), jnp.float32),
        ],
        name="mixer_scan",
    )(*projected, *constants)


def norm_kernel(turned, limit, gated, gain, out):
    owners, rows, width = gated.shape
    per_group = owners // GROUPS
    position = lax.broadcasted_iota(jnp.int32, (rows, 1), 0)
    valid = position < limit[0]
    for group in range(GROUPS):
        members = range(group * per_group, (group + 1) * per_group)
        squares = jnp.zeros((rows, width), jnp.float32)
        for owner in members:
            block = gated[owner].astype(jnp.float32)
            squares = squares + block * block
        mean = jnp.sum(squares, axis=1, keepdims=True) * (1.0 / (per_group * width))
        scale = jnp.where(valid, lax.rsqrt(mean + 1e-05), 0.0)
        for owner in members:
            block = gated[owner].astype(jnp.float32) * scale * gain[owner : owner + 1]
            block = jnp.where(valid, block, 0.0).astype(jnp.bfloat16)
            start = owner * width
            if owner % 2 == 0:
                out[:, start : start + width] = block
            else:
                out[:, start + turned : start + width] = block[:, : width - turned]
                out[:, start : start + turned] = block[:, width - turned :]


def norm(limit, gated, gain, turned):
    owners, rows, width = gated.shape
    return pl.pallas_call(
        functools.partial(norm_kernel, turned),
        in_specs=[
            pl.BlockSpec(memory_space=pltpu.SMEM),
            pl.BlockSpec(memory_space=pltpu.VMEM),
            pl.BlockSpec(memory_space=pltpu.VMEM),
        ],
        out_specs=pl.BlockSpec(memory_space=pltpu.VMEM),
        out_shape=jax.ShapeDtypeStruct((rows, owners * width), jnp.bfloat16),
        name="gated_norm",
    )(limit, gated, gain)


def around(block, axis, distance):
    size = lax.axis_size(axis)
    return lax.ppermute(block, axis, [(i, (i + distance) % size) for i in range(size)])


def gather_rows(block, axis):
    depth = block.shape[0]
    half = depth // 2
    behind, ahead = around(block, axis, 1), around(block, axis, -1)
    far = jnp.concatenate(
        [around(behind[:half], axis, 1), around(ahead[half:], axis, -1)], axis=0
    )
    me = lax.axis_index(axis)
    whole = jnp.zeros((4 * depth,) + block.shape[1:], block.dtype)
    for distance, part in ((0, block), (3, behind), (1, ahead), (2, far)):
        whole = lax.dynamic_update_slice(whole, part, ((me + distance) % 4 * depth, 0))
    return whole


def local(
    tokens,
    w_z,
    w_x,
    w_bc,
    w_dt,
    dt_bias,
    a_rate,
    conv_weight,
    conv_bias,
    d_skip,
    norm_gain,
    lengths,
):
    own_rows = tokens[0]
    num_rows, depth = own_rows.shape
    width = w_x.shape[1]
    me = lax.axis_index("seq")
    owners = lax.axis_size("seq")
    odd = me % 2 == 1
    chip_heads = 2 * width // HEAD
    turned = width - 3 * HEAD
    inner = norm_gain.shape[0]
    group = me // (owners // GROUPS)

    rows = num_rows // PIECES
    token_pieces = [
        lax.all_gather(own_rows[j * rows : (j + 1) * rows], "seq") for j in range(PIECES)
    ]

    def turn(columns):
        return jnp.where(odd, jnp.roll(columns, -turned, axis=-1), columns)

    def pad(array, size):
        return jnp.pad(array, ((0, 0), (0, size - array.shape[-1])))

    def heads_of(array):
        chip = lax.dynamic_slice_in_dim(array, me // 2 * chip_heads, chip_heads, -1)
        return jnp.where(
            odd, jnp.concatenate([chip[..., 4:7], chip[..., 3:4]], axis=-1), chip[..., :4]
        )

    def states_of(array, start):
        first = lax.dynamic_slice_in_dim(array, start + group * STATE, STATE, -1)
        second = lax.dynamic_slice_in_dim(
            array, start + (GROUPS + group) * STATE, STATE, -1
        )
        return first, second

    both = gather_rows(jnp.concatenate([turn(w_x), turn(w_z)], axis=1), "req")
    w_b, w_c = states_of(w_bc, 0)
    weights = jnp.concatenate(
        [
            pad(both[:, :width], SLOT),
            pad(both[:, width:], SLOT),
            pad(w_b, TILE),
            pad(jnp.concatenate([w_c, heads_of(w_dt)], axis=1), TILE),
        ],
        axis=1,
    )

    def channels_of(array):
        x_part = turn(lax.dynamic_slice_in_dim(array, me * width, width, -1))
        b_part, c_part = states_of(array, inner)
        return jnp.concatenate([pad(x_part, SLOT), pad(b_part, TILE), pad(c_part, TILE)], axis=1)

    taps = channels_of(conv_weight)
    bias = channels_of(conv_bias[None])
    head_rows = jnp.pad(
        jnp.stack([heads_of(dt_bias), heads_of(a_rate)]), ((0, 0), (STATE, TILE - STATE - 4))
    )
    skip = jnp.repeat(heads_of(d_skip), HEAD)[None]
    gains = norm_gain.reshape(owners, width)
    gains = jnp.where(
        (jnp.arange(owners) % 2 == 1)[:, None], jnp.roll(gains, -turned, axis=1), gains
    )

    projected = []
    for piece in token_pieces:
        block = jnp.dot(
            piece.reshape(owners * rows, depth), weights, preferred_element_type=jnp.float32
        ).astype(jnp.bfloat16)
        projected.append(block.reshape(owners, rows, -1))
    gated = scan(projected, taps, bias, head_rows, skip, width)
    mine = lax.all_to_all(gated, "seq", split_axis=0, concat_axis=0, tiled=True)
    limit = lengths - me * num_rows
    return norm(limit, mine, gains, turned)[None]


def solution(mesh):
    placed = (
        P("req", "seq", None),
        P("req", "seq"),
        P("req", "seq"),
        P(),
        P(),
        P(),
        P(),
        P(),
        P(),
        P(),
        P(),
        P("req"),
    )
    return jax.shard_map(
        local, mesh=mesh, in_specs=placed, out_specs=P("req", "seq", None), check_vma=False
    )
```

```python
import functools

import jax
import jax.numpy as jnp
from jax import lax
from jax.experimental import pallas as pl
from jax.experimental.pallas import tpu as pltpu
from jax.sharding import PartitionSpec as P

GROUPS = 2
STATE = 64
HEAD = 64
TILE = 128
SLOT = 256
SIDE = 4


def split(value):
    high = value.astype(jnp.bfloat16)
    return high, (value - high.astype(jnp.float32)).astype(jnp.bfloat16)


def matmul(a, b, dims=((1,), (0,))):
    return lax.dot_general(a, b, (dims, ((), ())), preferred_element_type=jnp.float32)


def scan_kernel(*refs):
    parity, first_own, first_other, second_own, second_other = refs[:5]
    taps, conv_bias, head_rows, skip, out, xbc, state = refs[5:]
    step = pl.program_id(0)
    rows = first_own.shape[2]
    own = rows * 2
    past = xbc.shape[0] - TILE

    @pl.when(step == 0)
    def _():
        xbc[...] = jnp.zeros_like(xbc)
        state[...] = jnp.zeros_like(state)

    @pl.when(step > 0)
    def _():
        xbc[0:past] = xbc[TILE : TILE + past]

    gates = []
    halves = ((first_own, first_other), (second_own, second_other))
    for core in range(2):
        for half, (mine, other) in enumerate(halves):
            block = jnp.where(
                parity[0] == core,
                mine[0, 0].astype(jnp.float32),
                other[0, 0].astype(jnp.float32),
            )
            start = past + core * own + half * rows
            xbc[start : start + rows, :SLOT] = block[:, :SLOT]
            xbc[start : start + rows, SLOT:] = block[:, 2 * SLOT :]
            gates.append(block[:, SLOT : 2 * SLOT])
    gate = jnp.concatenate(gates, axis=0)

    total = conv_bias[...]
    count = taps.shape[0]
    for k in range(count):
        first = past - (count - 1) + k
        total = total + taps[k : k + 1] * xbc[first : first + TILE]
    conved = (total * jax.nn.sigmoid(total)).astype(jnp.bfloat16)
    b_proj = conved[:, SLOT : SLOT + TILE]
    c_proj = conved[:, SLOT + TILE :]

    raw = xbc[past : past + TILE, SLOT + TILE :]
    step_size = jax.nn.softplus(raw + head_rows[0:1])
    log_decay = -step_size * head_rows[1:2]
    row = lax.broadcasted_iota(jnp.int32, (TILE, TILE), 0)
    lane = lax.broadcasted_iota(jnp.int32, (TILE, TILE), 1)
    causal = row >= lane
    running = jnp.dot(
        causal.astype(jnp.float32),
        log_decay,
        precision=lax.Precision.HIGHEST,
        preferred_element_type=jnp.float32,
    )
    running_rows = running.T
    step_rows = step_size.T
    affinity = jnp.where(causal, matmul(c_proj, b_proj, ((1,), (1,))), 0.0)
    before = state[...]
    before_high, before_low = split(before)
    carried = matmul(c_proj, before_high) + matmul(c_proj, before_low)

    left = lane < HEAD
    for tile in range(SLOT // TILE):
        span = slice(tile * TILE, (tile + 1) * TILE)
        x = conved[:, span]
        mixing, columns, steps = [], [], []
        for half in range(2):
            at = STATE + 2 * tile + half
            column = jnp.broadcast_to(running[:, at : at + 1], (TILE, TILE))
            decay = jnp.exp(jnp.minimum(column - running_rows[at : at + 1], 0.0))
            mixing.append(decay * affinity * step_rows[at : at + 1])
            columns.append(column)
            steps.append(jnp.broadcast_to(step_size[:, at : at + 1], (TILE, TILE)))
        weights, rest = split(jnp.concatenate(mixing, axis=1))
        zero = jnp.zeros_like(x)
        values = jnp.concatenate([jnp.where(left, x, zero), jnp.where(left, zero, x)], axis=0)
        intra = matmul(weights, values) + matmul(rest, values)
        run = jnp.where(left, columns[0], columns[1])
        last = run[TILE - 1 :]
        x32 = x.astype(jnp.float32)
        result = intra + jnp.exp(run) * carried[:, span] + skip[:, span] * x32
        z = gate[:, span]
        gated = (result * (z * jax.nn.sigmoid(z))).astype(jnp.bfloat16)
        width = min(out.shape[2] - tile * TILE, TILE)
        for owner in range(TILE // own):
            out[owner, :, tile * TILE : tile * TILE + width] = gated[
                owner * own : (owner + 1) * own, :width
            ]
        added = x32 * (jnp.exp(last - run) * jnp.where(left, steps[0], steps[1]))
        added_high, added_low = split(added)
        block = matmul(b_proj, added_high, ((0,), (0,))) + matmul(b_proj, added_low, ((0,), (0,)))
        state[:, span] = jnp.exp(last) * before[:, span] + block


def scan(parity, projected, taps, conv_bias, head_rows, skip, width):
    _, _, rows, columns = projected[0].shape
    own = rows * 2
    per_step = 2
    owners = per_step * SIDE * SIDE
    by_y = pl.BlockSpec((1, 1, rows, columns), lambda i: (i % SIDE, i // SIDE, 0, 0))
    by_x = pl.BlockSpec((1, 1, rows, columns), lambda i: (i // SIDE, i % SIDE, 0, 0))
    whole = lambda array: pl.BlockSpec(array.shape, lambda i: (0,) * array.ndim)
    constants = (taps, conv_bias, head_rows, skip)
    return pl.pallas_call(
        scan_kernel,
        grid=(owners // per_step,),
        in_specs=[pl.BlockSpec(memory_space=pltpu.SMEM), by_y, by_y, by_x, by_x]
        + [whole(array) for array in constants],
        out_specs=pl.BlockSpec((per_step, own, width), lambda i: (i, 0, 0)),
        out_shape=jax.ShapeDtypeStruct((owners, own, width), jnp.bfloat16),
        scratch_shapes=[
            pltpu.VMEM((TILE + 8, 2 * SLOT), jnp.float32),
            pltpu.VMEM((TILE, SLOT), jnp.float32),
        ],
        name="mixer_scan",
    )(parity, *projected, *constants)


def norm_kernel(turned, limit, gated, gain, out):
    owners, rows, width = gated.shape
    per_group = owners // GROUPS
    position = lax.broadcasted_iota(jnp.int32, (rows, 1), 0)
    valid = position < limit[0]
    for group in range(GROUPS):
        members = range(group * per_group, (group + 1) * per_group)
        squares = jnp.zeros((rows, width), jnp.float32)
        for owner in members:
            block = gated[owner].astype(jnp.float32)
            squares = squares + block * block
        mean = jnp.sum(squares, axis=1, keepdims=True) * (1.0 / (per_group * width))
        scale = jnp.where(valid, lax.rsqrt(mean + 1e-05), 0.0)
        for owner in members:
            block = gated[owner].astype(jnp.float32) * scale * gain[owner : owner + 1]
            block = jnp.where(valid, block, 0.0).astype(jnp.bfloat16)
            start = owner * width
            if owner % 2 == 0:
                out[:, start : start + width] = block
            else:
                out[:, start + turned : start + width] = block[:, : width - turned]
                out[:, start : start + turned] = block[:, width - turned :]


def norm(limit, gated, gain, turned):
    owners, rows, width = gated.shape
    return pl.pallas_call(
        functools.partial(norm_kernel, turned),
        in_specs=[
            pl.BlockSpec(memory_space=pltpu.SMEM),
            pl.BlockSpec(memory_space=pltpu.VMEM),
            pl.BlockSpec(memory_space=pltpu.VMEM),
        ],
        out_specs=pl.BlockSpec(memory_space=pltpu.VMEM),
        out_shape=jax.ShapeDtypeStruct((rows, owners * width), jnp.bfloat16),
        name="gated_norm",
    )(limit, gated, gain)


def around(block, axis, distance):
    size = lax.axis_size(axis)
    return lax.ppermute(block, axis, [(i, (i + distance) % size) for i in range(size)])


def gather_rows(block, axis):
    depth = block.shape[0]
    half = depth // 2
    behind, ahead = around(block, axis, 1), around(block, axis, -1)
    far = jnp.concatenate(
        [around(behind[:half], axis, 1), around(ahead[half:], axis, -1)], axis=0
    )
    me = lax.axis_index(axis)
    whole = jnp.zeros((4 * depth,) + block.shape[1:], block.dtype)
    for distance, part in ((0, block), (3, behind), (1, ahead), (2, far)):
        whole = lax.dynamic_update_slice(whole, part, ((me + distance) % 4 * depth, 0))
    return whole


def move(block, dx, dy, across=0):
    pairs = []
    for x in range(SIDE):
        for y in range(SIDE):
            for core in range(2):
                target = ((x + dx) % SIDE * SIDE + (y + dy) % SIDE) * 2 + (core + across) % 2
                pairs.append(((x * SIDE + y) * 2 + core, target))
    return lax.ppermute(block, "seq", pairs)


def line(block, dx, dy):
    half = block.shape[0] // 2
    behind, ahead = move(block, dx, dy), move(block, -dx, -dy)
    far = jnp.concatenate(
        [move(behind[:half], dx, dy), move(ahead[half:], -dx, -dy)], axis=0
    )
    return block, ahead, far, behind


def place(parts, position):
    rows = parts[0].shape[0]
    whole = jnp.zeros((SIDE * rows,) + parts[0].shape[1:], parts[0].dtype)
    for distance, part in enumerate(parts):
        whole = lax.dynamic_update_slice(whole, part, ((position + distance) % SIDE * rows, 0))
    return whole


def local(
    tokens,
    w_z,
    w_x,
    w_bc,
    w_dt,
    dt_bias,
    a_rate,
    conv_weight,
    conv_bias,
    d_skip,
    norm_gain,
    lengths,
):
    own_rows = tokens[0]
    num_rows, depth = own_rows.shape
    width = w_x.shape[1]
    me = lax.axis_index("seq")
    owners = lax.axis_size("seq")
    odd = me % 2 == 1
    chip_heads = 2 * width // HEAD
    turned = width - 3 * HEAD
    inner = norm_gain.shape[0]
    group = me // (owners // GROUPS)

    at_x, at_y = me // (2 * SIDE), me // 2 % SIDE
    rows = num_rows // 2
    column = place(line(own_rows[:rows], 1, 0), at_x)
    row = place(line(own_rows[rows:], 0, 1), at_y)
    first_parts = line(column, 0, 1)
    second_parts = line(row, 1, 0)

    def turn(columns):
        return jnp.where(odd, jnp.roll(columns, -turned, axis=-1), columns)

    def pad(array, size):
        return jnp.pad(array, ((0, 0), (0, size - array.shape[-1])))

    def heads_of(array):
        chip = lax.dynamic_slice_in_dim(array, me // 2 * chip_heads, chip_heads, -1)
        return jnp.where(
            odd, jnp.concatenate([chip[..., 4:7], chip[..., 3:4]], axis=-1), chip[..., :4]
        )

    def states_of(array, start):
        first = lax.dynamic_slice_in_dim(array, start + group * STATE, STATE, -1)
        second = lax.dynamic_slice_in_dim(
            array, start + (GROUPS + group) * STATE, STATE, -1
        )
        return first, second

    both = gather_rows(jnp.concatenate([turn(w_x), turn(w_z)], axis=1), "req")
    w_b, w_c = states_of(w_bc, 0)
    weights = jnp.concatenate(
        [
            pad(both[:, :width], SLOT),
            pad(both[:, width:], SLOT),
            pad(w_b, TILE),
            pad(jnp.concatenate([w_c, heads_of(w_dt)], axis=1), TILE),
        ],
        axis=1,
    )

    def channels_of(array):
        x_part = turn(lax.dynamic_slice_in_dim(array, me * width, width, -1))
        b_part, c_part = states_of(array, inner)
        return jnp.concatenate([pad(x_part, SLOT), pad(b_part, TILE), pad(c_part, TILE)], axis=1)

    taps = channels_of(conv_weight)
    bias = channels_of(conv_bias[None])
    head_rows = jnp.pad(
        jnp.stack([heads_of(dt_bias), heads_of(a_rate)]), ((0, 0), (STATE, TILE - STATE - 4))
    )
    skip = jnp.repeat(heads_of(d_skip), HEAD)[None]
    gains = norm_gain.reshape(owners, width)
    gains = jnp.where(
        (jnp.arange(owners) % 2 == 1)[:, None], jnp.roll(gains, -turned, axis=1), gains
    )

    def project(parts, position):
        blocks = [
            jnp.dot(part, weights, preferred_element_type=jnp.float32).astype(jnp.bfloat16)
            for part in parts
        ]
        return place(blocks, position).reshape(SIDE, SIDE, rows, -1)

    projected = []
    for parts, position in ((first_parts, at_y), (second_parts, at_x)):
        projected.append(project(parts, position))
        projected.append(project([move(part, 0, 0, 1) for part in parts], position))
    parity = (me % 2)[None]
    gated = scan(parity, projected, taps, bias, head_rows, skip, width)
    mine = lax.all_to_all(gated, "seq", split_axis=0, concat_axis=0, tiled=True)
    limit = lengths - me * num_rows
    return norm(limit, mine, gains, turned)[None]


def solution(mesh):
    placed = (
        P("req", "seq", None),
        P("req", "seq"),
        P("req", "seq"),
        P(),
        P(),
        P(),
        P(),
        P(),
        P(),
        P(),
        P(),
        P("req"),
    )
    return jax.shard_map(
        local, mesh=mesh, in_specs=placed, out_specs=P("req", "seq", None), check_vma=False
    )
```

```python
import functools

import jax
import jax.numpy as jnp
from jax import lax
from jax.experimental import pallas as pl
from jax.experimental.pallas import tpu as pltpu
from jax.sharding import PartitionSpec as P

GROUPS = 2
STATE = 64
HEAD = 64
TILE = 128
SLOT = 256
SIDE = 4


def split(value):
    high = value.astype(jnp.bfloat16)
    return high, (value - high.astype(jnp.float32)).astype(jnp.bfloat16)


def matmul(a, b, dims=((1,), (0,))):
    return lax.dot_general(a, b, (dims, ((), ())), preferred_element_type=jnp.float32)


def scan_kernel(*refs):
    parity, first, second_own, second_other = refs[:4]
    taps, conv_bias, head_rows, skip, out, xbc, state = refs[4:]
    step = pl.program_id(0)
    rows = first.shape[1]
    own = rows * 2
    past = xbc.shape[0] - TILE

    @pl.when(step == 0)
    def _():
        xbc[...] = jnp.zeros_like(xbc)
        state[...] = jnp.zeros_like(state)

    @pl.when(step > 0)
    def _():
        xbc[0:past] = xbc[TILE : TILE + past]

    gates = []
    own_half = second_own[0].astype(jnp.float32)
    other_half = second_other[0].astype(jnp.float32)
    for core in range(2):
        second = jnp.where(parity[0] == core, own_half, other_half)
        for half, block in enumerate((first[core].astype(jnp.float32), second)):
            start = past + core * own + half * rows
            xbc[start : start + rows, :SLOT] = block[:, :SLOT]
            xbc[start : start + rows, SLOT:] = block[:, 2 * SLOT :]
            gates.append(block[:, SLOT : 2 * SLOT])
    gate = jnp.concatenate(gates, axis=0)

    total = conv_bias[...]
    count = taps.shape[0]
    for k in range(count):
        first = past - (count - 1) + k
        total = total + taps[k : k + 1] * xbc[first : first + TILE]
    conved = (total * jax.nn.sigmoid(total)).astype(jnp.bfloat16)
    b_proj = conved[:, SLOT : SLOT + TILE]
    c_proj = conved[:, SLOT + TILE :]

    raw = xbc[past : past + TILE, SLOT + TILE :]
    step_size = jax.nn.softplus(raw + head_rows[0:1])
    log_decay = -step_size * head_rows[1:2]
    row = lax.broadcasted_iota(jnp.int32, (TILE, TILE), 0)
    lane = lax.broadcasted_iota(jnp.int32, (TILE, TILE), 1)
    causal = row >= lane
    running = jnp.dot(
        causal.astype(jnp.float32),
        log_decay,
        precision=lax.Precision.HIGHEST,
        preferred_element_type=jnp.float32,
    )
    running_rows = running.T
    step_rows = step_size.T
    affinity = jnp.where(causal, matmul(c_proj, b_proj, ((1,), (1,))), 0.0)
    before = state[...]
    before_high, before_low = split(before)
    carried = matmul(c_proj, before_high) + matmul(c_proj, before_low)

    left = lane < HEAD
    for tile in range(SLOT // TILE):
        span = slice(tile * TILE, (tile + 1) * TILE)
        x = conved[:, span]
        mixing, columns, steps = [], [], []
        for half in range(2):
            at = STATE + 2 * tile + half
            column = jnp.broadcast_to(running[:, at : at + 1], (TILE, TILE))
            decay = jnp.exp(jnp.minimum(column - running_rows[at : at + 1], 0.0))
            mixing.append(decay * affinity * step_rows[at : at + 1])
            columns.append(column)
            steps.append(jnp.broadcast_to(step_size[:, at : at + 1], (TILE, TILE)))
        weights, rest = split(jnp.concatenate(mixing, axis=1))
        zero = jnp.zeros_like(x)
        values = jnp.concatenate([jnp.where(left, x, zero), jnp.where(left, zero, x)], axis=0)
        intra = matmul(weights, values) + matmul(rest, values)
        run = jnp.where(left, columns[0], columns[1])
        last = run[TILE - 1 :]
        x32 = x.astype(jnp.float32)
        result = intra + jnp.exp(run) * carried[:, span] + skip[:, span] * x32
        z = gate[:, span]
        gated = (result * (z * jax.nn.sigmoid(z))).astype(jnp.bfloat16)
        width = min(out.shape[2] - tile * TILE, TILE)
        for owner in range(TILE // own):
            out[owner, :, tile * TILE : tile * TILE + width] = gated[
                owner * own : (owner + 1) * own, :width
            ]
        added = x32 * (jnp.exp(last - run) * jnp.where(left, steps[0], steps[1]))
        added_high, added_low = split(added)
        block = matmul(b_proj, added_high, ((0,), (0,))) + matmul(b_proj, added_low, ((0,), (0,)))
        state[:, span] = jnp.exp(last) * before[:, span] + block


def scan(parity, projected, taps, conv_bias, head_rows, skip, width):
    first, second_own, second_other = projected
    owners, rows, columns = first.shape
    own = rows * 2
    per_step = 2
    by_device = pl.BlockSpec((per_step, rows, columns), lambda i: (i, 0, 0))
    by_chip = pl.BlockSpec((1, rows, columns), lambda i: (i, 0, 0))
    whole = lambda array: pl.BlockSpec(array.shape, lambda i: (0,) * array.ndim)
    constants = (taps, conv_bias, head_rows, skip)
    return pl.pallas_call(
        scan_kernel,
        grid=(owners // per_step,),
        in_specs=[pl.BlockSpec(memory_space=pltpu.SMEM), by_device, by_chip, by_chip]
        + [whole(array) for array in constants],
        out_specs=pl.BlockSpec((per_step, own, width), lambda i: (i, 0, 0)),
        out_shape=jax.ShapeDtypeStruct((owners, own, width), jnp.bfloat16),
        scratch_shapes=[
            pltpu.VMEM((TILE + 8, 2 * SLOT), jnp.float32),
            pltpu.VMEM((TILE, SLOT), jnp.float32),
        ],
        name="mixer_scan",
    )(parity, *projected, *constants)


def norm_kernel(turned, limit, gated, gain, out):
    owners, rows, width = gated.shape
    per_group = owners // GROUPS
    position = lax.broadcasted_iota(jnp.int32, (rows, 1), 0)
    valid = position < limit[0]
    for group in range(GROUPS):
        members = range(group * per_group, (group + 1) * per_group)
        squares = jnp.zeros((rows, width), jnp.float32)
        for owner in members:
            block = gated[owner].astype(jnp.float32)
            squares = squares + block * block
        mean = jnp.sum(squares, axis=1, keepdims=True) * (1.0 / (per_group * width))
        scale = jnp.where(valid, lax.rsqrt(mean + 1e-05), 0.0)
        for owner in members:
            block = gated[owner].astype(jnp.float32) * scale * gain[owner : owner + 1]
            block = jnp.where(valid, block, 0.0).astype(jnp.bfloat16)
            start = owner * width
            if owner % 2 == 0:
                out[:, start : start + width] = block
            else:
                out[:, start + turned : start + width] = block[:, : width - turned]
                out[:, start : start + turned] = block[:, width - turned :]


def norm(limit, gated, gain, turned):
    owners, rows, width = gated.shape
    return pl.pallas_call(
        functools.partial(norm_kernel, turned),
        in_specs=[
            pl.BlockSpec(memory_space=pltpu.SMEM),
            pl.BlockSpec(memory_space=pltpu.VMEM),
            pl.BlockSpec(memory_space=pltpu.VMEM),
        ],
        out_specs=pl.BlockSpec(memory_space=pltpu.VMEM),
        out_shape=jax.ShapeDtypeStruct((rows, owners * width), jnp.bfloat16),
        name="gated_norm",
    )(limit, gated, gain)


def around(block, axis, distance):
    size = lax.axis_size(axis)
    return lax.ppermute(block, axis, [(i, (i + distance) % size) for i in range(size)])


def gather_rows(block, axis):
    depth = block.shape[0]
    half = depth // 2
    behind, ahead = around(block, axis, 1), around(block, axis, -1)
    far = jnp.concatenate(
        [around(behind[:half], axis, 1), around(ahead[half:], axis, -1)], axis=0
    )
    me = lax.axis_index(axis)
    whole = jnp.zeros((4 * depth,) + block.shape[1:], block.dtype)
    for distance, part in ((0, block), (3, behind), (1, ahead), (2, far)):
        whole = lax.dynamic_update_slice(whole, part, ((me + distance) % 4 * depth, 0))
    return whole


def move(block, dx, dy, across=0):
    pairs = []
    for x in range(SIDE):
        for y in range(SIDE):
            for core in range(2):
                target = ((x + dx) % SIDE * SIDE + (y + dy) % SIDE) * 2 + (core + across) % 2
                pairs.append(((x * SIDE + y) * 2 + core, target))
    return lax.ppermute(block, "seq", pairs)


def line(block, dx, dy):
    half = block.shape[0] // 2
    behind, ahead = move(block, dx, dy), move(block, -dx, -dy)
    far = jnp.concatenate(
        [move(behind[:half], dx, dy), move(ahead[half:], -dx, -dy)], axis=0
    )
    return block, ahead, far, behind


def nothing(array):
    return jnp.minimum(jnp.abs(array[0, 0].astype(jnp.float32)), 0.0).astype(jnp.int32)


def place(parts, position):
    rows = parts[0].shape[0]
    whole = jnp.zeros((SIDE * rows,) + parts[0].shape[1:], parts[0].dtype)
    for distance, part in enumerate(parts):
        whole = lax.dynamic_update_slice(whole, part, ((position + distance) % SIDE * rows, 0))
    return whole


def local(
    tokens,
    w_z,
    w_x,
    w_bc,
    w_dt,
    dt_bias,
    a_rate,
    conv_weight,
    conv_bias,
    d_skip,
    norm_gain,
    lengths,
):
    own_rows = tokens[0]
    num_rows, depth = own_rows.shape
    width = w_x.shape[1]
    me = lax.axis_index("seq")
    owners = lax.axis_size("seq")
    odd = me % 2 == 1
    chip_heads = 2 * width // HEAD
    turned = width - 3 * HEAD
    inner = norm_gain.shape[0]

    at_x, at_y = me // (2 * SIDE), me // 2 % SIDE
    rows = num_rows // 2
    first = lax.all_gather(own_rows[:rows], "seq").reshape(owners * rows, depth)
    row = place(line(own_rows[rows:], 0, 1), at_y)
    second_parts = line(row, 1, 0)
    second_own = place(second_parts, at_x)
    second_other = move(second_own, 0, 0, 1)
    early = me + nothing(row)
    late = me + nothing(second_parts[1])

    def turn(columns):
        return jnp.where(odd, jnp.roll(columns, -turned, axis=-1), columns)

    def pad(array, size):
        return jnp.pad(array, ((0, 0), (0, size - array.shape[-1])))

    def heads_of(array, me=late):
        chip = lax.dynamic_slice_in_dim(array, me // 2 * chip_heads, chip_heads, -1)
        return jnp.where(
            odd, jnp.concatenate([chip[..., 4:7], chip[..., 3:4]], axis=-1), chip[..., :4]
        )

    def states_of(array, start, me=late):
        group = me // (owners // GROUPS)
        first = lax.dynamic_slice_in_dim(array, start + group * STATE, STATE, -1)
        second = lax.dynamic_slice_in_dim(
            array, start + (GROUPS + group) * STATE, STATE, -1
        )
        return first, second

    both = gather_rows(jnp.concatenate([turn(w_x), turn(w_z)], axis=1), "req")
    w_b, w_c = states_of(w_bc, 0, early)
    weights = jnp.concatenate(
        [
            pad(both[:, :width], SLOT),
            pad(both[:, width:], SLOT),
            pad(w_b, TILE),
            pad(jnp.concatenate([w_c, heads_of(w_dt, early)], axis=1), TILE),
        ],
        axis=1,
    )

    def channels_of(array):
        x_part = turn(lax.dynamic_slice_in_dim(array, late * width, width, -1))
        b_part, c_part = states_of(array, inner)
        return jnp.concatenate([pad(x_part, SLOT), pad(b_part, TILE), pad(c_part, TILE)], axis=1)

    taps = channels_of(conv_weight)
    bias = channels_of(conv_bias[None])
    head_rows = jnp.pad(
        jnp.stack([heads_of(dt_bias), heads_of(a_rate)]), ((0, 0), (STATE, TILE - STATE - 4))
    )
    skip = jnp.repeat(heads_of(d_skip), HEAD)[None]
    gains = norm_gain.reshape(owners, width)
    gains = jnp.where(
        (jnp.arange(owners) % 2 == 1)[:, None], jnp.roll(gains, -turned, axis=1), gains
    )

    projected = [
        jnp.dot(part, weights, preferred_element_type=jnp.float32)
        .astype(jnp.bfloat16)
        .reshape(-1, rows, weights.shape[1])
        for part in (first, second_own, second_other)
    ]
    parity = (me % 2)[None]
    gated = scan(parity, projected, taps, bias, head_rows, skip, width)
    mine = lax.all_to_all(gated, "seq", split_axis=0, concat_axis=0, tiled=True)
    limit = lengths - me * num_rows
    return norm(limit, mine, gains, turned)[None]


def solution(mesh):
    placed = (
        P("req", "seq", None),
        P("req", "seq"),
        P("req", "seq"),
        P(),
        P(),
        P(),
        P(),
        P(),
        P(),
        P(),
        P(),
        P("req"),
    )
    return jax.shard_map(
        local, mesh=mesh, in_specs=placed, out_specs=P("req", "seq", None), check_vma=False
    )
```

```python
import functools

import jax
import jax.numpy as jnp
from jax import lax
from jax.experimental import pallas as pl
from jax.experimental.pallas import tpu as pltpu
from jax.sharding import PartitionSpec as P

GROUPS = 2
STATE = 64
HEAD = 64
TILE = 128
SLOT = 256


def split(value):
    high = value.astype(jnp.bfloat16)
    return high, (value - high.astype(jnp.float32)).astype(jnp.bfloat16)


def matmul(a, b, dims=((1,), (0,))):
    return lax.dot_general(a, b, (dims, ((), ())), preferred_element_type=jnp.float32)


def scan_kernel(
    tokens, weights, taps, conv_bias, head_rows, skip, out, ahead, xbc, state, *, own
):
    step = pl.program_id(0)
    past = xbc.shape[0] - TILE

    @pl.when(step == 0)
    def _():
        ahead[...] = jnp.zeros_like(ahead)

    @pl.when(step <= 1)
    def _():
        xbc[...] = jnp.zeros_like(xbc)
        state[...] = jnp.zeros_like(state)

    @pl.when(step > 1)
    def _():
        xbc[0:past] = xbc[TILE : TILE + past]

    projected = ahead[...]
    xbc[past : past + TILE, :SLOT] = projected[:, :SLOT].astype(jnp.float32)
    xbc[past : past + TILE, SLOT:] = projected[:, 2 * SLOT :].astype(jnp.float32)
    gate = projected[:, SLOT : 2 * SLOT].astype(jnp.float32)
    ahead[...] = matmul(tokens[...], weights[...]).astype(jnp.bfloat16)

    total = conv_bias[...]
    count = taps.shape[0]
    for k in range(count):
        first = past - (count - 1) + k
        total = total + taps[k : k + 1] * xbc[first : first + TILE]
    conved = (total * jax.nn.sigmoid(total)).astype(jnp.bfloat16)
    b_proj = conved[:, SLOT : SLOT + TILE]
    c_proj = conved[:, SLOT + TILE :]

    raw = xbc[past : past + TILE, SLOT + TILE :]
    step_size = jax.nn.softplus(raw + head_rows[0:1])
    log_decay = -step_size * head_rows[1:2]
    row = lax.broadcasted_iota(jnp.int32, (TILE, TILE), 0)
    lane = lax.broadcasted_iota(jnp.int32, (TILE, TILE), 1)
    causal = row >= lane
    running = jnp.dot(
        causal.astype(jnp.float32),
        log_decay,
        precision=lax.Precision.HIGHEST,
        preferred_element_type=jnp.float32,
    )
    running_rows = running.T
    step_rows = step_size.T
    affinity = jnp.where(causal, matmul(c_proj, b_proj, ((1,), (1,))), 0.0)
    before = state[...]
    before_high, before_low = split(before)
    carried = matmul(c_proj, before_high) + matmul(c_proj, before_low)

    left = lane < HEAD
    for tile in range(SLOT // TILE):
        span = slice(tile * TILE, (tile + 1) * TILE)
        x = conved[:, span]
        mixing, columns, steps = [], [], []
        for half in range(2):
            at = STATE + 2 * tile + half
            column = jnp.broadcast_to(running[:, at : at + 1], (TILE, TILE))
            decay = jnp.exp(jnp.minimum(column - running_rows[at : at + 1], 0.0))
            mixing.append(decay * affinity * step_rows[at : at + 1])
            columns.append(column)
            steps.append(jnp.broadcast_to(step_size[:, at : at + 1], (TILE, TILE)))
        weights, rest = split(jnp.concatenate(mixing, axis=1))
        zero = jnp.zeros_like(x)
        values = jnp.concatenate([jnp.where(left, x, zero), jnp.where(left, zero, x)], axis=0)
        intra = matmul(weights, values) + matmul(rest, values)
        run = jnp.where(left, columns[0], columns[1])
        last = run[TILE - 1 :]
        x32 = x.astype(jnp.float32)
        result = intra + jnp.exp(run) * carried[:, span] + skip[:, span] * x32
        z = gate[:, span]
        gated = (result * (z * jax.nn.sigmoid(z))).astype(jnp.bfloat16)
        width = min(out.shape[2] - tile * TILE, TILE)
        for owner in range(TILE // own):
            out[owner, :, tile * TILE : tile * TILE + width] = gated[
                owner * own : (owner + 1) * own, :width
            ]
        added = x32 * (jnp.exp(last - run) * jnp.where(left, steps[0], steps[1]))
        added_high, added_low = split(added)
        block = matmul(b_proj, added_high, ((0,), (0,))) + matmul(b_proj, added_low, ((0,), (0,)))
        state[:, span] = jnp.exp(last) * before[:, span] + block


def scan(tokens, weights, taps, conv_bias, head_rows, skip, own, width):
    positions, depth = tokens.shape
    steps = positions // TILE
    per_step = TILE // own
    whole = lambda array: pl.BlockSpec(array.shape, lambda i: (0,) * array.ndim)
    constants = (weights, taps, conv_bias, head_rows, skip)
    return pl.pallas_call(
        functools.partial(scan_kernel, own=own),
        grid=(steps + 1,),
        in_specs=[pl.BlockSpec((TILE, depth), lambda i: (jnp.minimum(i, steps - 1), 0))]
        + [whole(array) for array in constants],
        out_specs=pl.BlockSpec((per_step, own, width), lambda i: (jnp.maximum(i - 1, 0), 0, 0)),
        out_shape=jax.ShapeDtypeStruct((positions // own, own, width), jnp.bfloat16),
        scratch_shapes=[
            pltpu.VMEM((TILE, weights.shape[1]), jnp.bfloat16),
            pltpu.VMEM((TILE + 8, 2 * SLOT), jnp.float32),
            pltpu.VMEM((TILE, SLOT), jnp.float32),
        ],
        name="mixer_scan",
    )(tokens, *constants)


def norm_kernel(turned, limit, gated, gain, out):
    owners, rows, width = gated.shape
    per_group = owners // GROUPS
    position = lax.broadcasted_iota(jnp.int32, (rows, 1), 0)
    valid = position < limit[0]
    for group in range(GROUPS):
        members = range(group * per_group, (group + 1) * per_group)
        squares = jnp.zeros((rows, width), jnp.float32)
        for owner in members:
            block = gated[owner].astype(jnp.float32)
            squares = squares + block * block
        mean = jnp.sum(squares, axis=1, keepdims=True) * (1.0 / (per_group * width))
        scale = jnp.where(valid, lax.rsqrt(mean + 1e-05), 0.0)
        for owner in members:
            block = gated[owner].astype(jnp.float32) * scale * gain[owner : owner + 1]
            block = jnp.where(valid, block, 0.0).astype(jnp.bfloat16)
            start = owner * width
            if owner % 2 == 0:
                out[:, start : start + width] = block
            else:
                out[:, start + turned : start + width] = block[:, : width - turned]
                out[:, start : start + turned] = block[:, width - turned :]


def norm(limit, gated, gain, turned):
    owners, rows, width = gated.shape
    return pl.pallas_call(
        functools.partial(norm_kernel, turned),
        in_specs=[
            pl.BlockSpec(memory_space=pltpu.SMEM),
            pl.BlockSpec(memory_space=pltpu.VMEM),
            pl.BlockSpec(memory_space=pltpu.VMEM),
        ],
        out_specs=pl.BlockSpec(memory_space=pltpu.VMEM),
        out_shape=jax.ShapeDtypeStruct((rows, owners * width), jnp.bfloat16),
        name="gated_norm",
    )(limit, gated, gain)


def around(block, axis, distance):
    size = lax.axis_size(axis)
    return lax.ppermute(block, axis, [(i, (i + distance) % size) for i in range(size)])


def gather_rows(block, axis):
    depth = block.shape[0]
    half = depth // 2
    behind, ahead = around(block, axis, 1), around(block, axis, -1)
    far = jnp.concatenate(
        [around(behind[:half], axis, 1), around(ahead[half:], axis, -1)], axis=0
    )
    me = lax.axis_index(axis)
    whole = jnp.zeros((4 * depth,) + block.shape[1:], block.dtype)
    for distance, part in ((0, block), (3, behind), (1, ahead), (2, far)):
        whole = lax.dynamic_update_slice(whole, part, ((me + distance) % 4 * depth, 0))
    return whole


def local(
    tokens,
    w_z,
    w_x,
    w_bc,
    w_dt,
    dt_bias,
    a_rate,
    conv_weight,
    conv_bias,
    d_skip,
    norm_gain,
    lengths,
):
    own_rows = tokens[0]
    num_rows, depth = own_rows.shape
    width = w_x.shape[1]
    me = lax.axis_index("seq")
    owners = lax.axis_size("seq")
    odd = me % 2 == 1
    chip_heads = 2 * width // HEAD
    turned = width - 3 * HEAD
    inner = norm_gain.shape[0]
    group = me // (owners // GROUPS)

    gathered = lax.all_gather(own_rows, "seq").reshape(owners * num_rows, depth)

    def turn(columns):
        return jnp.where(odd, jnp.roll(columns, -turned, axis=-1), columns)

    def pad(array, size):
        return jnp.pad(array, ((0, 0), (0, size - array.shape[-1])))

    def heads_of(array):
        chip = lax.dynamic_slice_in_dim(array, me // 2 * chip_heads, chip_heads, -1)
        return jnp.where(
            odd, jnp.concatenate([chip[..., 4:7], chip[..., 3:4]], axis=-1), chip[..., :4]
        )

    def states_of(array, start):
        first = lax.dynamic_slice_in_dim(array, start + group * STATE, STATE, -1)
        second = lax.dynamic_slice_in_dim(
            array, start + (GROUPS + group) * STATE, STATE, -1
        )
        return first, second

    both = gather_rows(jnp.concatenate([turn(w_x), turn(w_z)], axis=1), "req")
    w_b, w_c = states_of(w_bc, 0)
    weights = jnp.concatenate(
        [
            pad(both[:, :width], SLOT),
            pad(both[:, width:], SLOT),
            pad(w_b, TILE),
            pad(jnp.concatenate([w_c, heads_of(w_dt)], axis=1), TILE),
        ],
        axis=1,
    )

    def channels_of(array):
        x_part = turn(lax.dynamic_slice_in_dim(array, me * width, width, -1))
        b_part, c_part = states_of(array, inner)
        return jnp.concatenate([pad(x_part, SLOT), pad(b_part, TILE), pad(c_part, TILE)], axis=1)

    taps = channels_of(conv_weight)
    bias = channels_of(conv_bias[None])
    head_rows = jnp.pad(
        jnp.stack([heads_of(dt_bias), heads_of(a_rate)]), ((0, 0), (STATE, TILE - STATE - 4))
    )
    skip = jnp.repeat(heads_of(d_skip), HEAD)[None]
    gains = norm_gain.reshape(owners, width)
    gains = jnp.where(
        (jnp.arange(owners) % 2 == 1)[:, None], jnp.roll(gains, -turned, axis=1), gains
    )

    gated = scan(gathered, weights, taps, bias, head_rows, skip, num_rows, width)
    mine = lax.all_to_all(gated, "seq", split_axis=0, concat_axis=0, tiled=True)
    limit = lengths - me * num_rows
    return norm(limit, mine, gains, turned)[None]


def solution(mesh):
    placed = (
        P("req", "seq", None),
        P("req", "seq"),
        P("req", "seq"),
        P(),
        P(),
        P(),
        P(),
        P(),
        P(),
        P(),
        P(),
        P("req"),
    )
    return jax.shard_map(
        local, mesh=mesh, in_specs=placed, out_specs=P("req", "seq", None), check_vma=False
    )
```

```python
import functools

import jax
import jax.numpy as jnp
from jax import lax
from jax.experimental import pallas as pl
from jax.experimental.pallas import tpu as pltpu
from jax.sharding import PartitionSpec as P

GROUPS = 2
STATE = 64
HEAD = 64
TILE = 128
AHEAD = 256
SLOT = 256


def split(value):
    high = value.astype(jnp.bfloat16)
    return high, (value - high.astype(jnp.float32)).astype(jnp.bfloat16)


def matmul(a, b, dims=((1,), (0,))):
    return lax.dot_general(a, b, (dims, ((), ())), preferred_element_type=jnp.float32)


def scan_kernel(
    tokens, weights, taps, conv_bias, head_rows, skip, out, ahead, xbc, state, *, own
):
    step = pl.program_id(0)
    past = xbc.shape[0] - TILE

    @pl.when(step == 0)
    def _():
        ahead[...] = jnp.zeros_like(ahead)

    @pl.when(step <= 1)
    def _():
        xbc[...] = jnp.zeros_like(xbc)
        state[...] = jnp.zeros_like(state)

    every = ahead[...]
    ahead[...] = matmul(tokens[...], weights[...]).astype(jnp.bfloat16)
    for part in range(AHEAD // TILE):
        xbc[0:past] = xbc[TILE : TILE + past]
        projected = every[part * TILE : (part + 1) * TILE]
        xbc[past : past + TILE, :SLOT] = projected[:, :SLOT].astype(jnp.float32)
        xbc[past : past + TILE, SLOT:] = projected[:, 2 * SLOT :].astype(jnp.float32)
        gate = projected[:, SLOT : 2 * SLOT].astype(jnp.float32)

        total = conv_bias[...]
        count = taps.shape[0]
        for k in range(count):
            first = past - (count - 1) + k
            total = total + taps[k : k + 1] * xbc[first : first + TILE]
        conved = (total * jax.nn.sigmoid(total)).astype(jnp.bfloat16)
        b_proj = conved[:, SLOT : SLOT + TILE]
        c_proj = conved[:, SLOT + TILE :]

        raw = xbc[past : past + TILE, SLOT + TILE :]
        step_size = jax.nn.softplus(raw + head_rows[0:1])
        log_decay = -step_size * head_rows[1:2]
        row = lax.broadcasted_iota(jnp.int32, (TILE, TILE), 0)
        lane = lax.broadcasted_iota(jnp.int32, (TILE, TILE), 1)
        causal = row >= lane
        running = jnp.dot(
            causal.astype(jnp.float32),
            log_decay,
            precision=lax.Precision.HIGHEST,
            preferred_element_type=jnp.float32,
        )
        running_rows = running.T
        step_rows = step_size.T
        affinity = jnp.where(causal, matmul(c_proj, b_proj, ((1,), (1,))), 0.0)
        before = state[...]
        before_high, before_low = split(before)
        carried = matmul(c_proj, before_high) + matmul(c_proj, before_low)

        left = lane < HEAD
        for tile in range(SLOT // TILE):
            span = slice(tile * TILE, (tile + 1) * TILE)
            x = conved[:, span]
            mixing, columns, steps = [], [], []
            for half in range(2):
                at = STATE + 2 * tile + half
                column = jnp.broadcast_to(running[:, at : at + 1], (TILE, TILE))
                decay = jnp.exp(jnp.minimum(column - running_rows[at : at + 1], 0.0))
                mixing.append(decay * affinity * step_rows[at : at + 1])
                columns.append(column)
                steps.append(jnp.broadcast_to(step_size[:, at : at + 1], (TILE, TILE)))
            weights, rest = split(jnp.concatenate(mixing, axis=1))
            zero = jnp.zeros_like(x)
            values = jnp.concatenate([jnp.where(left, x, zero), jnp.where(left, zero, x)], axis=0)
            intra = matmul(weights, values) + matmul(rest, values)
            run = jnp.where(left, columns[0], columns[1])
            last = run[TILE - 1 :]
            x32 = x.astype(jnp.float32)
            result = intra + jnp.exp(run) * carried[:, span] + skip[:, span] * x32
            z = gate[:, span]
            gated = (result * (z * jax.nn.sigmoid(z))).astype(jnp.bfloat16)
            width = min(out.shape[2] - tile * TILE, TILE)
            for owner in range(TILE // own):
                out[part * (TILE // own) + owner, :, tile * TILE : tile * TILE + width] = gated[
                    owner * own : (owner + 1) * own, :width
                ]
            added = x32 * (jnp.exp(last - run) * jnp.where(left, steps[0], steps[1]))
            added_high, added_low = split(added)
            block = matmul(b_proj, added_high, ((0,), (0,))) + matmul(b_proj, added_low, ((0,), (0,)))
            state[:, span] = jnp.exp(last) * before[:, span] + block


def scan(tokens, weights, taps, conv_bias, head_rows, skip, own, width):
    positions, depth = tokens.shape
    steps = positions // AHEAD
    per_step = AHEAD // own
    whole = lambda array: pl.BlockSpec(array.shape, lambda i: (0,) * array.ndim)
    constants = (weights, taps, conv_bias, head_rows, skip)
    return pl.pallas_call(
        functools.partial(scan_kernel, own=own),
        grid=(steps + 1,),
        in_specs=[pl.BlockSpec((AHEAD, depth), lambda i: (jnp.minimum(i, steps - 1), 0))]
        + [whole(array) for array in constants],
        out_specs=pl.BlockSpec((per_step, own, width), lambda i: (jnp.maximum(i - 1, 0), 0, 0)),
        out_shape=jax.ShapeDtypeStruct((positions // own, own, width), jnp.bfloat16),
        scratch_shapes=[
            pltpu.VMEM((AHEAD, weights.shape[1]), jnp.bfloat16),
            pltpu.VMEM((TILE + 8, 2 * SLOT), jnp.float32),
            pltpu.VMEM((TILE, SLOT), jnp.float32),
        ],
        name="mixer_scan",
    )(tokens, *constants)


def norm_kernel(turned, limit, gated, gain, out):
    owners, rows, width = gated.shape
    per_group = owners // GROUPS
    position = lax.broadcasted_iota(jnp.int32, (rows, 1), 0)
    valid = position < limit[0]
    for group in range(GROUPS):
        members = range(group * per_group, (group + 1) * per_group)
        squares = jnp.zeros((rows, width), jnp.float32)
        for owner in members:
            block = gated[owner].astype(jnp.float32)
            squares = squares + block * block
        mean = jnp.sum(squares, axis=1, keepdims=True) * (1.0 / (per_group * width))
        scale = jnp.where(valid, lax.rsqrt(mean + 1e-05), 0.0)
        for owner in members:
            block = gated[owner].astype(jnp.float32) * scale * gain[owner : owner + 1]
            block = jnp.where(valid, block, 0.0).astype(jnp.bfloat16)
            start = owner * width
            if owner % 2 == 0:
                out[:, start : start + width] = block
            else:
                out[:, start + turned : start + width] = block[:, : width - turned]
                out[:, start : start + turned] = block[:, width - turned :]


def norm(limit, gated, gain, turned):
    owners, rows, width = gated.shape
    return pl.pallas_call(
        functools.partial(norm_kernel, turned),
        in_specs=[
            pl.BlockSpec(memory_space=pltpu.SMEM),
            pl.BlockSpec(memory_space=pltpu.VMEM),
            pl.BlockSpec(memory_space=pltpu.VMEM),
        ],
        out_specs=pl.BlockSpec(memory_space=pltpu.VMEM),
        out_shape=jax.ShapeDtypeStruct((rows, owners * width), jnp.bfloat16),
        name="gated_norm",
    )(limit, gated, gain)


def around(block, axis, distance):
    size = lax.axis_size(axis)
    return lax.ppermute(block, axis, [(i, (i + distance) % size) for i in range(size)])


def gather_rows(block, axis):
    depth = block.shape[0]
    half = depth // 2
    behind, ahead = around(block, axis, 1), around(block, axis, -1)
    far = jnp.concatenate(
        [around(behind[:half], axis, 1), around(ahead[half:], axis, -1)], axis=0
    )
    me = lax.axis_index(axis)
    whole = jnp.zeros((4 * depth,) + block.shape[1:], block.dtype)
    for distance, part in ((0, block), (3, behind), (1, ahead), (2, far)):
        whole = lax.dynamic_update_slice(whole, part, ((me + distance) % 4 * depth, 0))
    return whole


def local(
    tokens,
    w_z,
    w_x,
    w_bc,
    w_dt,
    dt_bias,
    a_rate,
    conv_weight,
    conv_bias,
    d_skip,
    norm_gain,
    lengths,
):
    own_rows = tokens[0]
    num_rows, depth = own_rows.shape
    width = w_x.shape[1]
    me = lax.axis_index("seq")
    owners = lax.axis_size("seq")
    odd = me % 2 == 1
    chip_heads = 2 * width // HEAD
    turned = width - 3 * HEAD
    inner = norm_gain.shape[0]
    group = me // (owners // GROUPS)

    gathered = lax.all_gather(own_rows, "seq").reshape(owners * num_rows, depth)

    def turn(columns):
        return jnp.where(odd, jnp.roll(columns, -turned, axis=-1), columns)

    def pad(array, size):
        return jnp.pad(array, ((0, 0), (0, size - array.shape[-1])))

    def heads_of(array):
        chip = lax.dynamic_slice_in_dim(array, me // 2 * chip_heads, chip_heads, -1)
        return jnp.where(
            odd, jnp.concatenate([chip[..., 4:7], chip[..., 3:4]], axis=-1), chip[..., :4]
        )

    def states_of(array, start):
        first = lax.dynamic_slice_in_dim(array, start + group * STATE, STATE, -1)
        second = lax.dynamic_slice_in_dim(
            array, start + (GROUPS + group) * STATE, STATE, -1
        )
        return first, second

    both = gather_rows(jnp.concatenate([turn(w_x), turn(w_z)], axis=1), "req")
    w_b, w_c = states_of(w_bc, 0)
    weights = jnp.concatenate(
        [
            pad(both[:, :width], SLOT),
            pad(both[:, width:], SLOT),
            pad(w_b, TILE),
            pad(jnp.concatenate([w_c, heads_of(w_dt)], axis=1), TILE),
        ],
        axis=1,
    )

    def channels_of(array):
        x_part = turn(lax.dynamic_slice_in_dim(array, me * width, width, -1))
        b_part, c_part = states_of(array, inner)
        return jnp.concatenate([pad(x_part, SLOT), pad(b_part, TILE), pad(c_part, TILE)], axis=1)

    taps = channels_of(conv_weight)
    bias = channels_of(conv_bias[None])
    head_rows = jnp.pad(
        jnp.stack([heads_of(dt_bias), heads_of(a_rate)]), ((0, 0), (STATE, TILE - STATE - 4))
    )
    skip = jnp.repeat(heads_of(d_skip), HEAD)[None]
    gains = norm_gain.reshape(owners, width)
    gains = jnp.where(
        (jnp.arange(owners) % 2 == 1)[:, None], jnp.roll(gains, -turned, axis=1), gains
    )

    gated = scan(gathered, weights, taps, bias, head_rows, skip, num_rows, width)
    mine = lax.all_to_all(gated, "seq", split_axis=0, concat_axis=0, tiled=True)
    limit = lengths - me * num_rows
    return norm(limit, mine, gains, turned)[None]


def solution(mesh):
    placed = (
        P("req", "seq", None),
        P("req", "seq"),
        P("req", "seq"),
        P(),
        P(),
        P(),
        P(),
        P(),
        P(),
        P(),
        P(),
        P("req"),
    )
    return jax.shard_map(
        local, mesh=mesh, in_specs=placed, out_specs=P("req", "seq", None), check_vma=False
    )
```
